128 devices in a mesh: dp: 16 (over z, x), mp: 8 (over y, core).
Axes of the slice: x: 4, y: 4, z: 4, core: 2. Of those that a mesh axis runs over, the one named last changes fastest.
Arguments:
- stats: float32 [8, 128, 256, 256], P('mp', 'dp'), may hold values from -1 to 1, as said below
- prev_roots: float32 [8, 128, 256, 256], P('mp', 'dp'), may hold values from -1 to 2, as said below
- counts: int32 [8, 16], replicated, may hold values from 1 to 8, as said below
- grads: bfloat16 [8, 128, 256, 2048], P(None, 'dp', None, 'mp'), may hold values from -6 to 6
Outputs:
- precond: bfloat16 [8, 128, 256, 2048], P(None, 'dp', None, 'mp')
The draws below stay inside these ranges and needn't reach their ends.
Inputs may be any that keep to these rules, and one draw needn't show every extreme that they name: Each model shard's live blocks are the first count slots of each of its devices; every count is 1 to 8, 8 is reached on some device, and the counts of one model shard sum to at most 64, which some model shard reaches. `stats`: every block is symmetric positive definite. `prev_roots`: every block is symmetric.
All inputs are finite; a program needn't handle non-finite values.
Results may differ from the reference program's by a relative error of at most 0.0052.
Values may be sent and summed in bfloat16 or wider, within the bound.
No kernel may reach another device: no remote copies, remote signals or barrier semaphores. Data moves between devices by JAX's collectives and lax.ppermute only.
A program may use at most 128 MiB of HBM per device.

```python
import math
import jax
import jax.numpy as jnp
from jax import lax

B = 256
NEWTON = 2
SLOT = 8
SHARE = 4
OWNERS = 8
WORKERS = 16


def symmetric_noise(noise_key, block_shape, spread):
    values = jnp.clip(jax.random.normal(noise_key, block_shape, jnp.float32), -4.0, 4.0)
    return (values + jnp.swapaxes(values, -1, -2)) * (spread / math.sqrt(2.0 * B))


def draw_stats(key, part):
    block_shape = (OWNERS, WORKERS * SLOT, B, B)
    first_key, second_key = jax.random.split(jax.random.fold_in(key, 101))
    noise_part = symmetric_noise(first_key, block_shape, 0.25)
    scales = jnp.exp(jax.random.uniform(second_key, block_shape[:-1], jnp.float32, math.log(0.8), math.log(1.25)))
    identity = jnp.eye(B, dtype=jnp.float32)
    return 0.4 * scales[..., :, None] * (identity + noise_part) * scales[..., None, :]


def draw_prev_roots(key, part):
    block_shape = (OWNERS, WORKERS * SLOT, B, B)
    noise_part = symmetric_noise(jax.random.fold_in(key, 202), block_shape, 0.2)
    return jnp.eye(B, dtype=jnp.float32) + noise_part


def draw_counts(key, part):
    key_list = jax.random.split(jax.random.fold_in(key, 303), 4)
    spare_units = (SHARE - 1) * WORKERS
    full_row = jax.random.randint(key_list[0], (), 0, OWNERS)
    extra_units = jax.random.randint(key_list[1], (OWNERS,), 3 * spare_units // 4, spare_units + 1)
    is_full = jnp.arange(OWNERS) == full_row
    extra_units = jnp.where(is_full, spare_units, extra_units)
    favoured = jax.random.randint(key_list[2], (OWNERS,), 0, WORKERS)
    unit_count = WORKERS * (SLOT - 1)
    scores = jax.random.randint(key_list[3], (OWNERS, WORKERS, SLOT - 1), 0, 65536)
    position = jnp.arange(unit_count, dtype=jnp.int32).reshape(1, WORKERS, SLOT - 1)
    boosted = (jnp.arange(WORKERS)[None, :, None] == favoured[:, None, None]) & is_full[:, None, None]
    scores = scores * unit_count + position + boosted.astype(jnp.int32) * (65536 * unit_count)
    flat_scores = scores.reshape(OWNERS, unit_count)
    ordering = jnp.argsort(-flat_scores, axis=1)
    unit_rank = jnp.argsort(ordering, axis=1)
    chosen = (unit_rank < extra_units[:, None]).astype(jnp.int32).reshape(OWNERS, WORKERS, SLOT - 1)
    return (1 + jnp.sum(chosen, axis=2)).astype(jnp.int32)


def levels(stream_key, extent, shards, least, largest):
    loudness = 1.0
    for axis_at, parts in shards:
        heights = jax.random.uniform(jax.random.fold_in(jax.random.fold_in(stream_key, 6), axis_at), (parts,), jnp.float32, least / len(shards), largest / len(shards))
        loudness = loudness * jnp.repeat(jnp.exp(heights), extent[axis_at] // parts).reshape((-1,) + (1,) * (len(extent) - 1 - axis_at))
    return loudness


def bell_draw(rng, extent, scale, reach, shards=(), kind=jnp.bfloat16):
    values = jax.random.normal(rng, extent, jnp.float32) * scale
    if len(shards) > 0:
        values = levels(rng, extent, shards, -0.22, 0.18) * values
    return jnp.clip(values, min=-reach, max=reach).astype(kind)


def setup_inputs(seed: int = 0) -> dict:
    seeds = jax.random.split(jax.random.key(seed), 5)
    stats = draw_stats(jax.random.fold_in(seeds[4], 71), 0)
    prev_roots = draw_prev_roots(jax.random.fold_in(seeds[4], 71), 0)
    counts = draw_counts(jax.random.fold_in(seeds[4], 71), 0)
    grads = bell_draw(seeds[3], (OWNERS, WORKERS * SLOT, B, OWNERS * B), 1.0, 6.0, ((1, 16), (3, 8)))
    return dict(stats=stats, prev_roots=prev_roots, counts=counts, grads=grads)


def product(left_side, right_side):
    return jnp.einsum("nij,njk->nik", left_side, right_side, precision=lax.Precision.HIGHEST)


def newton_root(statistic, initial):
    identity = jnp.eye(statistic.shape[-1], dtype=statistic.dtype)
    square = product(initial, initial)
    moment = product(product(square, square), statistic)
    estimate = initial
    for iteration in range(NEWTON):
        newton_step = (5.0 * identity - moment) * 0.25
        estimate = product(estimate, newton_step)
        if iteration + 1 < NEWTON:
            double = product(newton_step, newton_step)
            moment = product(product(double, double), moment)
    return estimate


def precondition_owner(paired):
    left_side = paired[0].astype(jnp.float32)
    right_side = paired[1].astype(jnp.float32)
    return jnp.einsum("gab,gbc->gac", left_side, right_side).astype(jnp.bfloat16)


def reference(stats, prev_roots, counts, grads):
    block_groups = OWNERS * WORKERS
    grouped = (stats.reshape(block_groups, SLOT, B, B), prev_roots.reshape(block_groups, SLOT, B, B))
    root_blocks = lax.map(lambda paired: newton_root(paired[0], paired[1]), grouped)
    live_mask = jnp.arange(SLOT, dtype=jnp.int32)[None, None, :] < counts[:, :, None]
    live_mask = live_mask.reshape(block_groups, SLOT, 1, 1)
    band_root = jnp.where(live_mask, root_blocks.astype(jnp.bfloat16), jnp.zeros((), jnp.bfloat16))
    band_root = band_root.reshape(OWNERS, WORKERS * SLOT, B, B)
    return lax.map(precondition_owner, (band_root, grads))
```

```python
import functools
import jax
import jax.numpy as jnp
from jax import lax
from jax.experimental import pallas as pl
from jax.experimental.pallas import tpu as pltpu
from jax.sharding import PartitionSpec as P

F32 = jnp.float32
BF16 = jnp.bfloat16
SMEM = pltpu.SMEM
VMEM = pltpu.VMEM


def dot(a, b):
    return jnp.dot(a.astype(BF16), b.astype(BF16), preferred_element_type=F32)


def newton(stats, starts, eye):
    n = [x - eye for x in starts]
    p = [2.0 * v + dot(v, v) for v in n]
    q = [2.0 * v + dot(v, v) for v in p]
    a = stats()
    m = [s + dot(v, s) for s, v in zip(a, q)]
    x = [1.25 * s - 0.25 * (u + dot(v, u)) for s, u, v in zip(starts, m, n)]
    e = [0.0625 * dot(v, v) - 0.625 * v for v in m]
    f = [3.125 * v + dot(v, v) for v in e]
    m = [2.44140625 * u + dot(v, u) for u, v in zip(m, f)]
    return [1.25 * v - 0.25 * (u + dot(v - eye, u)) for v, u in zip(x, m)]


def newton_kernel(first, stats, roots, out, abuf, xbuf, sems):
    size = out.shape[0]
    order = out.shape[-1]
    loads = [
        [pltpu.make_async_copy(src.at[0, first + i], buf.at[i], sems.at[w, i]) for i in range(size)]
        for w, (src, buf) in enumerate(((roots, xbuf), (stats, abuf)))
    ]
    for load in loads[0] + loads[1]:
        load.start()
    row = lax.broadcasted_iota(jnp.int32, (order, order), 0)
    col = lax.broadcasted_iota(jnp.int32, (order, order), 1)
    eye = (row == col).astype(F32)
    for load in loads[0]:
        load.wait()

    def late():
        for load in loads[1]:
            load.wait()
        return [abuf[i] for i in range(size)]

    for i, value in enumerate(newton(late, [xbuf[i] for i in range(size)], eye)):
        out[i] = value.astype(BF16)


def newton_call(stats, roots, first, size):
    order = stats.shape[-1]
    return pl.pallas_call(
        functools.partial(newton_kernel, first),
        out_shape=jax.ShapeDtypeStruct((size, order, order), BF16),
        in_specs=[pl.BlockSpec(memory_space=pltpu.HBM)] * 2,
        out_specs=pl.BlockSpec(memory_space=VMEM),
        scratch_shapes=[
            pltpu.VMEM((size, order, order), F32),
            pltpu.VMEM((size, order, order), F32),
            pltpu.SemaphoreType.DMA((2, size)),
        ],
        cost_estimate=pl.CostEstimate(
            flops=size * 16 * order**3, bytes_accessed=size * order * order * 10, transcendentals=0
        ),
        compiler_params=pltpu.CompilerParams(vmem_limit_bytes=16 << 20),
        name="newton",
    )(stats, roots)


def apply_kernel(spec, zeros, counts, grads, *refs):
    count = len(spec)
    blocks = refs[:count]
    out, gbuf, obuf, zbuf, gsem, osem, zsem = refs[-7:]
    me = lax.axis_index("mp")
    worker = lax.axis_index("dp")
    owners, slots = grads.shape[0], grads.shape[1]

    entries = []
    at = 0
    for ref, (shift, flip, first) in zip(blocks, spec):
        owner = lax.rem(me + shift, owners)
        if flip:
            owner = owner + 1 - 2 * lax.rem(owner, 2)
        live = counts[owner, worker]
        entries.append((ref, owner, first, live, at, ref.shape[0]))
        at += ref.shape[0]

    def load(owner, slot, i):
        return pltpu.make_async_copy(grads.at[owner, slot], gbuf.at[i], gsem.at[i])

    def store(owner, slot, i):
        return pltpu.make_async_copy(obuf.at[i], out.at[owner, slot], osem.at[i])

    def blank(owner, slot):
        return pltpu.make_async_copy(zbuf, out.at[owner, slot], zsem)

    flat = [
        (ref, k, owner, first + k, first + k < live, at + k)
        for ref, owner, first, live, at, size in entries
        for k in range(size)
    ]
    for _, _, owner, slot, live, i in flat:
        pl.when(live)(load(owner, slot, i).start)

    if zeros:
        zbuf[...] = jnp.zeros_like(zbuf)

        @pl.loop(0, owners)
        def _(m):
            @pl.loop(counts[m, worker], slots)
            def _(k):
                blank(m, k).start()

    for g in range(0, len(flat), 4):
        group = flat[g : g + 4]
        for _, _, owner, slot, live, i in group:
            pl.when(live)(load(owner, slot, i).wait)
        values = [dot(ref[k], gbuf[i]).astype(BF16) for ref, k, _, _, _, i in group]
        for (_, _, _, _, _, i), value in zip(group, values):
            obuf[i] = value
        for _, _, owner, slot, live, i in group:
            pl.when(live)(store(owner, slot, i).start)

    for _, _, owner, slot, live, i in flat:
        pl.when(live)(store(owner, slot, i).wait)

    if zeros:
        @pl.loop(0, owners)
        def _(m):
            @pl.loop(counts[m, worker], slots)
            def _(k):
                blank(m, k).wait()


def apply_call(counts, grads, pieces, result=None):
    spec = [piece[1:] for piece in pieces]
    blocks = [piece[0] for piece in pieces]
    total = sum(block.shape[0] for block in blocks)
    order = grads.shape[-1]
    out_shape = jax.ShapeDtypeStruct(grads.shape, BF16)
    anyspec = pl.BlockSpec(memory_space=pltpu.HBM)
    extra = [] if result is None else [result]

    def body(counts, grads, *refs):
        refs = refs[: len(blocks)] + refs[len(blocks) + len(extra) :]
        apply_kernel(spec, result is None, counts, grads, *refs)

    return pl.pallas_call(
        body,
        out_shape=out_shape,
        in_specs=[pl.BlockSpec(memory_space=SMEM), anyspec]
        + [pl.BlockSpec(memory_space=VMEM)] * len(blocks)
        + [anyspec] * len(extra),
        out_specs=anyspec,
        scratch_shapes=[
            pltpu.VMEM((total, order, order), BF16),
            pltpu.VMEM((total, order, order), BF16),
            pltpu.VMEM((order, order), BF16),
            pltpu.SemaphoreType.DMA((total,)),
            pltpu.SemaphoreType.DMA((total,)),
            pltpu.SemaphoreType.DMA,
        ],
        input_output_aliases={2 + len(blocks): 0} if extra else {},
        cost_estimate=pl.CostEstimate(
            flops=total * 2 * order**3, bytes_accessed=total * order * order * 4, transcendentals=0
        ),
        compiler_params=pltpu.CompilerParams(vmem_limit_bytes=16 << 20),
        name="apply",
    )(counts, grads, *blocks, *extra)


def local(size, stats, roots, counts, grads):
    up = [(i, (i + 2) % size) for i in range(size)]
    down = [(i, (i - 2) % size) for i in range(size)]
    core = [(i, i ^ 1) for i in range(size)]
    move = lambda block, pairs: lax.ppermute(block, "mp", pairs)
    after = lambda result, *values: lax.optimization_barrier((*values, result))
    slots = stats.shape[1]
    half = slots // 2
    ups, downs = size - 2, 2
    hbm = lambda value: pltpu.with_memory_space_constraint(value, pltpu.HBM)
    stats, roots, grads = hbm(stats), hbm(roots), hbm(grads)

    own_a = newton_call(stats, roots, 0, half)
    up_a, down_a = move(own_a, up), move(own_a, down)
    own_b = newton_call(stats, roots, half, slots - half)
    up_b, down_b = move(own_b, up), move(own_b, down)
    sib_a, sib_b = move(own_a, core), move(own_b, core)
    result = apply_call(counts, grads, [(own_a, 0, 0, 0), (own_b, 0, 0, half)])

    part = half // 2
    up_a, down_a, result = after(result, up_a, down_a)
    far_ua, far_da = move(up_a[:part], up), move(down_a[part:], down)
    x_up_a, x_down_a = move(up_a, core), move(down_a, core)
    result = apply_call(
        counts,
        grads,
        [(sib_a, 0, 1, 0), (sib_b, 0, 1, half), (up_a, ups, 0, 0), (down_a, downs, 0, 0)],
        result,
    )
    up_b, down_b, result = after(result, up_b, down_b)
    far_ub, far_db = move(up_b[:part], up), move(down_b[part:], down)
    x_up_b, x_down_b = move(up_b, core), move(down_b, core)
    result = apply_call(
        counts,
        grads,
        [
            (x_up_a, ups, 1, 0),
            (x_down_a, downs, 1, 0),
            (up_b, ups, 0, half),
            (down_b, downs, 0, half),
        ],
        result,
    )
    far_ua, far_da, result = after(result, far_ua, far_da)
    x_far_ua, x_far_da = move(far_ua, core), move(far_da, core)
    result = apply_call(
        counts,
        grads,
        [
            (x_up_b, ups, 1, half),
            (x_down_b, downs, 1, half),
            (far_ua, 4, 0, 0),
            (far_da, 4, 0, part),
            (x_far_ua, 4, 1, 0),
            (x_far_da, 4, 1, part),
        ],
        result,
    )
    far_ub, far_db, result = after(result, far_ub, far_db)
    x_far_ub, x_far_db = move(far_ub, core), move(far_db, core)
    return apply_call(
        counts,
        grads,
        [
            (far_ub, 4, 0, half),
            (far_db, 4, 0, half + part),
            (x_far_ub, 4, 1, half),
            (x_far_db, 4, 1, half + part),
        ],
        result,
    )


def solution(mesh):
    return jax.shard_map(
        functools.partial(local, mesh.shape["mp"]),
        mesh=mesh,
        in_specs=(
            P("mp", "dp", None, None),
            P("mp", "dp", None, None),
            P(),
            P(None, "dp", None, "mp"),
        ),
        out_specs=P(None, "dp", None, "mp"),
        check_vma=False,
    )
```

```python
import functools
import jax
import jax.numpy as jnp
from jax import lax
from jax.experimental import pallas as pl
from jax.experimental.pallas import tpu as pltpu
from jax.sharding import PartitionSpec as P

F32 = jnp.float32
BF16 = jnp.bfloat16
SMEM = pltpu.SMEM
VMEM = pltpu.VMEM


def dot(a, b):
    return jnp.dot(a.astype(BF16), b.astype(BF16), preferred_element_type=F32)


def newton(stats, starts, eye):
    n = [x - eye for x in starts]
    p = [2.0 * v + dot(v, v) for v in n]
    q = [2.0 * v + dot(v, v) for v in p]
    a = stats()
    m = [s + dot(v, s) for s, v in zip(a, q)]
    x = [1.25 * s - 0.25 * (u + dot(v, u)) for s, u, v in zip(starts, m, n)]
    e = [0.0625 * dot(v, v) - 0.625 * v for v in m]
    f = [3.125 * v + dot(v, v) for v in e]
    m = [2.44140625 * u + dot(v, u) for u, v in zip(m, f)]
    return [1.25 * v - 0.25 * (u + dot(v - eye, u)) for v, u in zip(x, m)]


def newton_kernel(first, stats, roots, *refs):
    counts, out = (refs[0], refs[1]) if first == 0 else (None, refs[0])
    abuf, xbuf, sems = refs[3:6] if first == 0 else refs[1:4]
    size, order = out.shape[0], out.shape[-1]
    loads = [
        [pltpu.make_async_copy(src.at[0, first + i], buf.at[i], sems.at[w, i]) for i in range(size)]
        for w, (src, buf) in enumerate(((roots, xbuf), (stats, abuf)))
    ]
    if first == 0:
        busiest, cbuf, csem = refs[2], refs[6], refs[7]
        fetch = pltpu.make_async_copy(counts, cbuf, csem)
        fetch.start()
    for load in loads[0] + loads[1]:
        load.start()
    row = lax.broadcasted_iota(jnp.int32, (order, order), 0)
    col = lax.broadcasted_iota(jnp.int32, (order, order), 1)
    eye = (row == col).astype(F32)
    if first == 0:
        fetch.wait()
        over = [jnp.maximum(cbuf[m : m + 1, :] - size, 0) for m in range(cbuf.shape[0])]
        pairs = [x + y for x, y in zip(over[::2], over[1::2])]
        busiest[0] = jnp.max(functools.reduce(jnp.maximum, pairs))
    for load in loads[0]:
        load.wait()

    def late():
        for load in loads[1]:
            load.wait()
        return [abuf[i] for i in range(size)]

    for i, value in enumerate(newton(late, [xbuf[i] for i in range(size)], eye)):
        out[i] = value.astype(BF16)


def newton_call(stats, roots, first, size, counts=None):
    order = stats.shape[-1]
    out_shape = [jax.ShapeDtypeStruct((size, order, order), BF16)]
    out_specs = [pl.BlockSpec(memory_space=VMEM)]
    scratch = [
        pltpu.VMEM((size, order, order), F32),
        pltpu.VMEM((size, order, order), F32),
        pltpu.SemaphoreType.DMA((2, size)),
    ]
    extra = []
    if first == 0:
        extra = [counts]
        out_shape.append(jax.ShapeDtypeStruct((1,), jnp.int32))
        out_specs.append(pl.BlockSpec(memory_space=SMEM))
        scratch += [pltpu.VMEM(counts.shape, jnp.int32), pltpu.SemaphoreType.DMA]
    return pl.pallas_call(
        functools.partial(newton_kernel, first),
        out_shape=out_shape,
        in_specs=[pl.BlockSpec(memory_space=pltpu.HBM)] * (2 + len(extra)),
        out_specs=out_specs,
        scratch_shapes=scratch,
        cost_estimate=pl.CostEstimate(
            flops=size * 16 * order**3, bytes_accessed=size * order * order * 10, transcendentals=0
        ),
        compiler_params=pltpu.CompilerParams(vmem_limit_bytes=16 << 20),
        name="newton",
    )(stats, roots, *extra)


def blank_kernel(counts, after, out, zbuf, sem):
    worker = lax.axis_index("dp")
    zbuf[...] = jnp.zeros_like(zbuf)

    def dead(act):
        @pl.loop(0, out.shape[0])
        def _(m):
            @pl.loop(counts[m, worker], out.shape[1])
            def _(k):
                act(pltpu.make_async_copy(zbuf, out.at[m, k], sem))

    dead(lambda copy: copy.start())
    dead(lambda copy: copy.wait())


def blank_call(counts, like, after):
    return pl.pallas_call(
        blank_kernel,
        out_shape=jax.ShapeDtypeStruct(like.shape, BF16),
        in_specs=[pl.BlockSpec(memory_space=SMEM), pl.BlockSpec(memory_space=pl.ANY)],
        out_specs=pl.BlockSpec(memory_space=pltpu.HBM),
        scratch_shapes=[pltpu.VMEM(like.shape[2:], BF16), pltpu.SemaphoreType.DMA],
        cost_estimate=pl.CostEstimate(flops=0, bytes_accessed=like.size, transcendentals=0),
        compiler_params=pltpu.CompilerParams(vmem_limit_bytes=4 << 20),
        name="blank",
    )(counts, after)


def surplus(counts, worker, owner, base, half, k):
    core = lax.rem(owner, 2)
    even = owner - core
    item = jnp.where(core == 1, (k + half) % (2 * half), k)
    first = jnp.maximum(counts[even, worker] - base, 0)
    second = jnp.maximum(counts[even + 1, worker] - base, 0)
    slot = base + jnp.where(item < first, item, item - first)
    return jnp.where(item < first, even, even + 1), slot, item < first + second


def pack_kernel(base, counts, own, twin, out):
    worker, me = lax.axis_index("dp"), lax.axis_index("mp")
    for k in range(out.shape[0]):
        owner, slot, _ = surplus(counts, worker, me, base, out.shape[0] // 2, k)
        at = jnp.clip(slot - base, 0, own.shape[0] - 1)

        @pl.when(owner == me)
        def _():
            out[k] = own[at]

        @pl.when(owner != me)
        def _():
            out[k] = twin[at]


def pack_call(counts, own, twin, base, room):
    return pl.pallas_call(
        functools.partial(pack_kernel, base),
        out_shape=jax.ShapeDtypeStruct((room,) + own.shape[1:], BF16),
        in_specs=[pl.BlockSpec(memory_space=SMEM)] + [pl.BlockSpec(memory_space=VMEM)] * 2,
        out_specs=pl.BlockSpec(memory_space=VMEM),
        cost_estimate=pl.CostEstimate(
            flops=0, bytes_accessed=2 * room * own.shape[1] * own.shape[2] * 2, transcendentals=0
        ),
        compiler_params=pltpu.CompilerParams(vmem_limit_bytes=8 << 20),
        name="pack",
    )(counts, own, twin)


def apply_kernel(spec, stream, counts, grads, *refs):
    count = len(spec)
    blocks = refs[:count]
    out, obuf, osem = refs[count : count + 3]
    me = lax.axis_index("mp")
    worker = lax.axis_index("dp")
    owners, slots = grads.shape[0], grads.shape[1]
    core = lax.rem(me, 2)
    flat = []
    for ref, (hops, flip, swap, first, half) in zip(blocks, spec):
        side = 1 - core if flip else core
        owner = me - core + side + lax.rem(2 * owners + hops * 2 * (2 * side - 1), owners)
        owner = jnp.where(owner >= owners, owner - owners, owner)
        if swap:
            owner = owner + 1 - 2 * lax.rem(owner, 2)
        for k in range(ref.shape[0]):
            if half:
                source, slot, live = surplus(counts, worker, owner, first, half, k)
                slot = jnp.minimum(slot, slots - 1)
            else:
                source, slot = owner, first + k
                live = slot < counts[owner, worker]
            flat.append((ref, k, source, slot, live, len(flat)))

    def store(owner, slot, i):
        return pltpu.make_async_copy(obuf.at[i], out.at[owner, slot], osem.at[i])

    if stream:
        gbuf, gsem = refs[count + 3 :]

        def load(owner, slot, i):
            return pltpu.make_async_copy(grads.at[owner, slot], gbuf.at[i], gsem.at[i])

        for _, _, owner, slot, live, i in flat:
            pl.when(live)(load(owner, slot, i).start)

    for g in range(0, len(flat), 4):
        group = flat[g : g + 4]
        if stream:
            for _, _, owner, slot, live, i in group:
                pl.when(live)(load(owner, slot, i).wait)
        values = [
            dot(ref[k], gbuf[i] if stream else grads[owner, slot]).astype(BF16)
            for ref, k, owner, slot, _, i in group
        ]
        for (_, _, _, _, _, i), value in zip(group, values):
            obuf[i] = value
        for _, _, owner, slot, live, i in group:
            pl.when(live)(store(owner, slot, i).start)

    for _, _, owner, slot, live, i in flat:
        pl.when(live)(store(owner, slot, i).wait)


def apply_call(counts, grads, pieces, result, stream=False):
    spec = [piece[1:] for piece in pieces]
    blocks = [piece[0] for piece in pieces]
    total = sum(block.shape[0] for block in blocks)
    order = grads.shape[-1]
    anyspec = pl.BlockSpec(memory_space=pltpu.HBM)
    buffers = [pltpu.VMEM((total, order, order), BF16), pltpu.SemaphoreType.DMA((total,))]

    def body(counts, grads, *refs):
        refs = refs[: len(blocks)] + refs[len(blocks) + 1 :]
        apply_kernel(spec, stream, counts, grads, *refs)

    return pl.pallas_call(
        body,
        out_shape=jax.ShapeDtypeStruct(grads.shape, BF16),
        in_specs=[pl.BlockSpec(memory_space=SMEM), anyspec if stream else pl.BlockSpec(memory_space=VMEM)]
        + [pl.BlockSpec(memory_space=VMEM)] * len(blocks)
        + [anyspec],
        out_specs=anyspec,
        scratch_shapes=buffers * (2 if stream else 1),
        input_output_aliases={2 + len(blocks): 0},
        cost_estimate=pl.CostEstimate(
            flops=total * 2 * order**3, bytes_accessed=total * order * order * 4, transcendentals=0
        ),
        compiler_params=pltpu.CompilerParams(vmem_limit_bytes=16 << 20),
        name="apply",
    )(counts, grads, *blocks, result)


def spread(size, half, own_a, stats, roots, counts, grads):
    ring = [(i, (i + 2 - 4 * (i % 2)) % size) for i in range(size)]
    pair = [(i, i ^ 1) for i in range(size)]

    def move(block, pairs, name):
        with jax.named_scope("s_" + name):
            return lax.ppermute(block, "mp", pairs)

    base = own_a.shape[0]
    join = jnp.concatenate
    tie = lambda *values: lax.optimization_barrier(values)
    near_a = move(own_a, ring, "near_a")
    twin_a = move(own_a, pair, "twin_a")
    near_b = move(twin_a, ring, "near_b")
    own_b, = newton_call(stats, roots, base, stats.shape[1] - base)
    twin_b = move(own_b, pair, "twin_b")
    near_a, own_b, twin_b = tie(near_a, own_b, twin_b)
    extra = pack_call(counts, own_b, twin_b, base, 2 * half)
    near_c = move(extra, ring, "near_c")
    result = blank_call(counts, grads, extra)
    near_b, own_b, far_in = tie(near_b, own_b, near_a)
    far_a = move(far_in, ring, "far_a")
    twin_near = move(far_in, pair, "twin_near")
    result = apply_call(
        counts,
        grads,
        [
            (own_a, 0, 0, 0, 0, 0),
            (own_b, 0, 0, 0, base, 0),
            (twin_a, 0, 1, 0, 0, 0),
            (twin_b, 0, 1, 0, base, 0),
        ],
        result,
        True,
    )
    near_c, far_a, twin_near, result = tie(near_c, far_a, twin_near, result)
    far_c = move(near_c[:half], ring, "far_c")
    twin_c = move(join([near_b, near_c, far_a]), pair, "twin_c")
    result = apply_call(
        counts,
        grads,
        [
            (near_a, 1, 0, 0, 0, 0),
            (near_b, 1, 0, 1, 0, 0),
            (near_c, 1, 0, 0, base, half),
            (far_a, 2, 0, 0, 0, 0),
            (twin_near, 1, 1, 0, 0, 0),
        ],
        result,
    )
    twin_c, result = tie(twin_c, result)
    result = apply_call(
        counts,
        grads,
        [
            (twin_c[:base], 1, 1, 1, 0, 0),
            (twin_c[base : base + 2 * half], 1, 1, 0, base, half),
            (twin_c[base + 2 * half :], 2, 1, 0, 0, 0),
        ],
        result,
    )
    far_c, result = tie(far_c, result)
    twin_far = move(far_c, pair, "twin_far")
    return apply_call(
        counts, grads, [(far_c, 2, 0, 0, base, half), (twin_far, 2, 1, 0, base, half)], result
    )


def local(size, stats, roots, counts, grads):
    hbm = lambda value: pltpu.with_memory_space_constraint(value, pltpu.HBM)
    stats, roots = hbm(stats), hbm(roots)
    base = stats.shape[1] // 2
    own_a, busiest = newton_call(stats, roots, 0, base, counts)
    halves = (2, 3, 4)
    branches = [functools.partial(spread, size, half) for half in halves]
    index = sum((busiest[0] > 2 * half).astype(jnp.int32) for half in halves[:-1])
    return lax.switch(index, branches, own_a, stats, roots, counts, grads)


def solution(mesh):
    return jax.shard_map(
        functools.partial(local, mesh.shape["mp"]),
        mesh=mesh,
        in_specs=(
            P("mp", "dp", None, None),
            P("mp", "dp", None, None),
            P(),
            P(None, "dp", None, "mp"),
        ),
        out_specs=P(None, "dp", None, "mp"),
        check_vma=False,
    )
```

```python
import functools
import jax
import jax.numpy as jnp
from jax import lax
from jax.experimental import pallas as pl
from jax.experimental.pallas import tpu as pltpu
from jax.sharding import PartitionSpec as P

F32 = jnp.float32
BF16 = jnp.bfloat16
SMEM = pltpu.SMEM
VMEM = pltpu.VMEM


def dot(a, b):
    return jnp.dot(a.astype(BF16), b.astype(BF16), preferred_element_type=F32)


def newton(stats, starts, eye):
    n = [x - eye for x in starts]
    p = [2.0 * v + dot(v, v) for v in n]
    q = [2.0 * v + dot(v, v) for v in p]
    a = stats()
    m = [s + dot(v, s) for s, v in zip(a, q)]
    x = [1.25 * s - 0.25 * (u + dot(v, u)) for s, u, v in zip(starts, m, n)]
    e = [0.0625 * dot(v, v) - 0.625 * v for v in m]
    f = [3.125 * v + dot(v, v) for v in e]
    m = [2.44140625 * u + dot(v, u) for u, v in zip(m, f)]
    return [1.25 * v - 0.25 * (u + dot(v - eye, u)) for v, u in zip(x, m)]


def newton_kernel(first, stats, roots, *refs):
    counts, out = (refs[0], refs[1]) if first == 0 else (None, refs[0])
    abuf, xbuf, sems = refs[3:6] if first == 0 else refs[1:4]
    size, order = out.shape[0], out.shape[-1]
    loads = [
        [pltpu.make_async_copy(src.at[0, first + i], buf.at[i], sems.at[w, i]) for i in range(size)]
        for w, (src, buf) in enumerate(((roots, xbuf), (stats, abuf)))
    ]
    if first == 0:
        busiest, cbuf, csem = refs[2], refs[6], refs[7]
        fetch = pltpu.make_async_copy(counts, cbuf, csem)
        fetch.start()
    for load in loads[0] + loads[1]:
        load.start()
    row = lax.broadcasted_iota(jnp.int32, (order, order), 0)
    col = lax.broadcasted_iota(jnp.int32, (order, order), 1)
    eye = (row == col).astype(F32)
    if first == 0:
        fetch.wait()
        over = [jnp.maximum(cbuf[m : m + 1, :] - size, 0) for m in range(cbuf.shape[0])]
        pairs = [x + y for x, y in zip(over[::2], over[1::2])]
        busiest[0] = jnp.max(functools.reduce(jnp.maximum, pairs))
    for load in loads[0]:
        load.wait()

    def late():
        for load in loads[1]:
            load.wait()
        return [abuf[i] for i in range(size)]

    for i, value in enumerate(newton(late, [xbuf[i] for i in range(size)], eye)):
        out[i] = value.astype(BF16)


def newton_call(stats, roots, first, size, counts=None):
    order = stats.shape[-1]
    out_shape = [jax.ShapeDtypeStruct((size, order, order), BF16)]
    out_specs = [pl.BlockSpec(memory_space=VMEM)]
    scratch = [
        pltpu.VMEM((size, order, order), F32),
        pltpu.VMEM((size, order, order), F32),
        pltpu.SemaphoreType.DMA((2, size)),
    ]
    extra = []
    if first == 0:
        extra = [counts]
        out_shape.append(jax.ShapeDtypeStruct((1,), jnp.int32))
        out_specs.append(pl.BlockSpec(memory_space=SMEM))
        scratch += [pltpu.VMEM(counts.shape, jnp.int32), pltpu.SemaphoreType.DMA]
    return pl.pallas_call(
        functools.partial(newton_kernel, first),
        out_shape=out_shape,
        in_specs=[pl.BlockSpec(memory_space=pltpu.HBM)] * (2 + len(extra)),
        out_specs=out_specs,
        scratch_shapes=scratch,
        cost_estimate=pl.CostEstimate(
            flops=size * 16 * order**3, bytes_accessed=size * order * order * 10, transcendentals=0
        ),
        compiler_params=pltpu.CompilerParams(vmem_limit_bytes=16 << 20),
        name="newton",
    )(stats, roots, *extra)


def blank_kernel(counts, after, out, zbuf, sem):
    worker = lax.axis_index("dp")
    zbuf[...] = jnp.zeros_like(zbuf)

    def dead(act):
        @pl.loop(0, out.shape[0])
        def _(m):
            @pl.loop(counts[m, worker], out.shape[1])
            def _(k):
                act(pltpu.make_async_copy(zbuf, out.at[m, k], sem))

    dead(lambda copy: copy.start())
    dead(lambda copy: copy.wait())


def blank_call(counts, like, after):
    return pl.pallas_call(
        blank_kernel,
        out_shape=jax.ShapeDtypeStruct(like.shape, BF16),
        in_specs=[pl.BlockSpec(memory_space=SMEM), pl.BlockSpec(memory_space=pl.ANY)],
        out_specs=pl.BlockSpec(memory_space=pltpu.HBM),
        scratch_shapes=[pltpu.VMEM(like.shape[2:], BF16), pltpu.SemaphoreType.DMA],
        cost_estimate=pl.CostEstimate(flops=0, bytes_accessed=like.size, transcendentals=0),
        compiler_params=pltpu.CompilerParams(vmem_limit_bytes=4 << 20),
        name="blank",
    )(counts, after)


def surplus(counts, worker, owner, base, half, k):
    core = lax.rem(owner, 2)
    even = owner - core
    item = jnp.where(core == 1, (k + half) % (2 * half), k)
    first = jnp.maximum(counts[even, worker] - base, 0)
    second = jnp.maximum(counts[even + 1, worker] - base, 0)
    slot = base + jnp.where(item < first, item, item - first)
    return jnp.where(item < first, even, even + 1), slot, item < first + second


def pack_kernel(base, counts, own, twin, out):
    worker, me = lax.axis_index("dp"), lax.axis_index("mp")
    for k in range(out.shape[0]):
        owner, slot, _ = surplus(counts, worker, me, base, out.shape[0] // 2, k)
        at = jnp.clip(slot - base, 0, own.shape[0] - 1)

        @pl.when(owner == me)
        def _():
            out[k] = own[at]

        @pl.when(owner != me)
        def _():
            out[k] = twin[at]


def pack_call(counts, own, twin, base, room):
    return pl.pallas_call(
        functools.partial(pack_kernel, base),
        out_shape=jax.ShapeDtypeStruct((room,) + own.shape[1:], BF16),
        in_specs=[pl.BlockSpec(memory_space=SMEM)] + [pl.BlockSpec(memory_space=VMEM)] * 2,
        out_specs=pl.BlockSpec(memory_space=VMEM),
        cost_estimate=pl.CostEstimate(
            flops=0, bytes_accessed=2 * room * own.shape[1] * own.shape[2] * 2, transcendentals=0
        ),
        compiler_params=pltpu.CompilerParams(vmem_limit_bytes=8 << 20),
        name="pack",
    )(counts, own, twin)


def apply_kernel(spec, stream, counts, grads, *refs):
    count = len(spec)
    blocks = refs[:count]
    out, obuf, osem = refs[count : count + 3]
    me = lax.axis_index("mp")
    worker = lax.axis_index("dp")
    owners, slots = grads.shape[0], grads.shape[1]
    core = lax.rem(me, 2)
    flat = []
    for ref, (hops, flip, swap, first, half) in zip(blocks, spec):
        side = 1 - core if flip else core
        owner = me - core + side + lax.rem(2 * owners + hops * 2 * (2 * side - 1), owners)
        owner = jnp.where(owner >= owners, owner - owners, owner)
        if swap:
            owner = owner + 1 - 2 * lax.rem(owner, 2)
        for k in range(ref.shape[0]):
            if half:
                source, slot, live = surplus(counts, worker, owner, first, half, k)
                slot = jnp.minimum(slot, slots - 1)
            else:
                source, slot = owner, first + k
                live = slot < counts[owner, worker]
            flat.append((ref, k, source, slot, live, len(flat)))

    def store(owner, slot, i):
        return pltpu.make_async_copy(obuf.at[i], out.at[owner, slot], osem.at[i])

    if stream:
        gbuf, gsem = refs[count + 3 :]

        def load(owner, slot, i):
            return pltpu.make_async_copy(grads.at[owner, slot], gbuf.at[i], gsem.at[i])

        for _, _, owner, slot, live, i in flat:
            pl.when(live)(load(owner, slot, i).start)

    for g in range(0, len(flat), 4):
        group = flat[g : g + 4]
        if stream:
            for _, _, owner, slot, live, i in group:
                pl.when(live)(load(owner, slot, i).wait)
        values = [
            dot(ref[k], gbuf[i] if stream else grads[owner, slot]).astype(BF16)
            for ref, k, owner, slot, _, i in group
        ]
        for (_, _, _, _, _, i), value in zip(group, values):
            obuf[i] = value
        for _, _, owner, slot, live, i in group:
            pl.when(live)(store(owner, slot, i).start)

    for _, _, owner, slot, live, i in flat:
        pl.when(live)(store(owner, slot, i).wait)


def apply_call(counts, grads, pieces, result, stream=False):
    spec = [piece[1:] for piece in pieces]
    blocks = [piece[0] for piece in pieces]
    total = sum(block.shape[0] for block in blocks)
    order = grads.shape[-1]
    anyspec = pl.BlockSpec(memory_space=pltpu.HBM)
    buffers = [pltpu.VMEM((total, order, order), BF16), pltpu.SemaphoreType.DMA((total,))]

    def body(counts, grads, *refs):
        refs = refs[: len(blocks)] + refs[len(blocks) + 1 :]
        apply_kernel(spec, stream, counts, grads, *refs)

    return pl.pallas_call(
        body,
        out_shape=jax.ShapeDtypeStruct(grads.shape, BF16),
        in_specs=[pl.BlockSpec(memory_space=SMEM), anyspec if stream else pl.BlockSpec(memory_space=VMEM)]
        + [pl.BlockSpec(memory_space=VMEM)] * len(blocks)
        + [anyspec],
        out_specs=anyspec,
        scratch_shapes=buffers * (2 if stream else 1),
        input_output_aliases={2 + len(blocks): 0},
        cost_estimate=pl.CostEstimate(
            flops=total * 2 * order**3, bytes_accessed=total * order * order * 4, transcendentals=0
        ),
        compiler_params=pltpu.CompilerParams(vmem_limit_bytes=16 << 20),
        name="apply",
    )(counts, grads, *blocks, result)


def spread(size, half, own_a, stats, roots, counts, grads):
    ring = [(i, (i + 2 - 4 * (i % 2)) % size) for i in range(size)]
    pair = [(i, i ^ 1) for i in range(size)]

    def move(block, pairs, name):
        with jax.named_scope("s_" + name):
            return lax.ppermute(block, "mp", pairs)

    base = own_a.shape[0]
    join = jnp.concatenate
    tie = lambda *values: lax.optimization_barrier(values)
    near_a = move(own_a, ring, "near_a")
    twin_a = move(own_a, pair, "twin_a")
    near_b = move(twin_a, ring, "near_b")
    own_b, = newton_call(stats, roots, base, stats.shape[1] - base)
    twin_b = move(own_b, pair, "twin_b")
    near_a, own_b, twin_b = tie(near_a, own_b, twin_b)
    extra = pack_call(counts, own_b, twin_b, base, 2 * half)
    near_c = move(extra, ring, "near_c")
    result = blank_call(counts, grads, extra)
    near_b, own_b, far_in = tie(near_b, own_b, near_a)
    result = apply_call(
        counts,
        grads,
        [
            (own_a, 0, 0, 0, 0, 0),
            (own_b, 0, 0, 0, base, 0),
            (twin_a, 0, 1, 0, 0, 0),
            (twin_b, 0, 1, 0, base, 0),
        ],
        result,
        True,
    )
    near_c, result = tie(near_c, result)
    far = move(join([near_a, near_c[:half]]), ring, "far")
    twin_c = move(join([near_a, near_b, near_c]), pair, "twin_c")
    result = apply_call(
        counts,
        grads,
        [
            (near_a, 1, 0, 0, 0, 0),
            (near_b, 1, 0, 1, 0, 0),
            (near_c, 1, 0, 0, base, half),
            (twin_c[:base], 1, 1, 0, 0, 0),
            (twin_c[base : 2 * base], 1, 1, 1, 0, 0),
            (twin_c[2 * base :], 1, 1, 0, base, half),
        ],
        result,
    )
    far, result = tie(far, result)
    twin_far = move(far, pair, "twin_far")
    result = apply_call(counts, grads, [(far[:base], 2, 0, 0, 0, 0), (far[base:], 2, 0, 0, base, half)], result)
    return apply_call(
        counts, grads, [(twin_far[:base], 2, 1, 0, 0, 0), (twin_far[base:], 2, 1, 0, base, half)], result
    )


def local(size, stats, roots, counts, grads):
    hbm = lambda value: pltpu.with_memory_space_constraint(value, pltpu.HBM)
    stats, roots = hbm(stats), hbm(roots)
    base = stats.shape[1] // 2
    own_a, busiest = newton_call(stats, roots, 0, base, counts)
    halves = (2, 3, 4)
    branches = [functools.partial(spread, size, half) for half in halves]
    index = sum((busiest[0] > 2 * half).astype(jnp.int32) for half in halves[:-1])
    return lax.switch(index, branches, own_a, stats, roots, counts, grads)


def solution(mesh):
    return jax.shard_map(
        functools.partial(local, mesh.shape["mp"]),
        mesh=mesh,
        in_specs=(
            P("mp", "dp", None, None),
            P("mp", "dp", None, None),
            P(),
            P(None, "dp", None, "mp"),
        ),
        out_specs=P(None, "dp", None, "mp"),
        check_vma=False,
    )
```

```python
import functools
import jax
import jax.numpy as jnp
from jax import lax
from jax.experimental import pallas as pl
from jax.experimental.pallas import tpu as pltpu
from jax.sharding import PartitionSpec as P

F32 = jnp.float32
BF16 = jnp.bfloat16
SMEM = pltpu.SMEM
VMEM = pltpu.VMEM


def dot(a, b):
    return jnp.dot(a.astype(BF16), b.astype(BF16), preferred_element_type=F32)


def newton(stats, starts, eye):
    n, q, found = [], [], []
    for part in starts:
        values = part()
        shifted = [x - eye for x in values]
        p = [2.0 * v + dot(v, v) for v in shifted]
        q += [2.0 * v + dot(v, v) for v in p]
        n += shifted
        found += values
    starts = found
    a = stats()
    m = [s + dot(v, s) for s, v in zip(a, q)]
    x = [1.25 * s - 0.25 * (u + dot(v, u)) for s, u, v in zip(starts, m, n)]
    e = [0.0625 * dot(v, v) - 0.625 * v for v in m]
    f = [3.125 * v + dot(v, v) for v in e]
    m = [2.44140625 * u + dot(v, u) for u, v in zip(m, f)]
    return [1.25 * v - 0.25 * (u + dot(v - eye, u)) for v, u in zip(x, m)]


def newton_kernel(first, stats, roots, *refs):
    counts, out = (refs[0], refs[1]) if first == 0 else (None, refs[0])
    abuf, xbuf, sems = refs[3:6] if first == 0 else refs[1:4]
    size, order = out.shape[0], out.shape[-1]
    loads = [
        [pltpu.make_async_copy(src.at[0, first + i], buf.at[i], sems.at[w, i]) for i in range(size)]
        for w, (src, buf) in enumerate(((roots, xbuf), (stats, abuf)))
    ]
    if first == 0:
        busiest, cbuf, csem = refs[2], refs[6], refs[7]
        fetch = pltpu.make_async_copy(counts, cbuf, csem)
        fetch.start()
    for load in loads[0] + loads[1]:
        load.start()
    row = lax.broadcasted_iota(jnp.int32, (order, order), 0)
    col = lax.broadcasted_iota(jnp.int32, (order, order), 1)
    eye = (row == col).astype(F32)
    if first == 0:
        fetch.wait()
        over = [jnp.maximum(cbuf[m : m + 1, :] - size, 0) for m in range(cbuf.shape[0])]
        pairs = [x + y for x, y in zip(over[::2], over[1::2])]
        busiest[0] = jnp.max(functools.reduce(jnp.maximum, pairs))
    def early(i):
        for load in loads[0][i : i + 2]:
            load.wait()
        return [xbuf[k] for k in range(i, i + 2)]

    def late():
        for load in loads[1]:
            load.wait()
        return [abuf[i] for i in range(size)]

    for i, value in enumerate(newton(late, [functools.partial(early, i) for i in range(0, size, 2)], eye)):
        out[i] = value.astype(BF16)


def newton_call(stats, roots, first, size, counts=None):
    order = stats.shape[-1]
    out_shape = [jax.ShapeDtypeStruct((size, order, order), BF16)]
    out_specs = [pl.BlockSpec(memory_space=VMEM)]
    scratch = [
        pltpu.VMEM((size, order, order), F32),
        pltpu.VMEM((size, order, order), F32),
        pltpu.SemaphoreType.DMA((2, size)),
    ]
    extra = []
    if first == 0:
        extra = [counts]
        out_shape.append(jax.ShapeDtypeStruct((1,), jnp.int32))
        out_specs.append(pl.BlockSpec(memory_space=SMEM))
        scratch += [pltpu.VMEM(counts.shape, jnp.int32), pltpu.SemaphoreType.DMA]
    return pl.pallas_call(
        functools.partial(newton_kernel, first),
        out_shape=out_shape,
        in_specs=[pl.BlockSpec(memory_space=pltpu.HBM)] * (2 + len(extra)),
        out_specs=out_specs,
        scratch_shapes=scratch,
        cost_estimate=pl.CostEstimate(
            flops=size * 16 * order**3, bytes_accessed=size * order * order * 10, transcendentals=0
        ),
        compiler_params=pltpu.CompilerParams(vmem_limit_bytes=16 << 20),
        name="newton",
    )(stats, roots, *extra)


def blank_kernel(counts, after, out, zbuf, sem):
    worker = lax.axis_index("dp")
    zbuf[...] = jnp.zeros_like(zbuf)

    def dead(act):
        @pl.loop(0, out.shape[0])
        def _(m):
            @pl.loop(counts[m, worker], out.shape[1])
            def _(k):
                act(pltpu.make_async_copy(zbuf, out.at[m, k], sem))

    dead(lambda copy: copy.start())
    dead(lambda copy: copy.wait())


def blank_call(counts, like, after):
    return pl.pallas_call(
        blank_kernel,
        out_shape=jax.ShapeDtypeStruct(like.shape, BF16),
        in_specs=[pl.BlockSpec(memory_space=SMEM), pl.BlockSpec(memory_space=pl.ANY)],
        out_specs=pl.BlockSpec(memory_space=pltpu.HBM),
        scratch_shapes=[pltpu.VMEM(like.shape[2:], BF16), pltpu.SemaphoreType.DMA],
        cost_estimate=pl.CostEstimate(flops=0, bytes_accessed=like.size, transcendentals=0),
        compiler_params=pltpu.CompilerParams(vmem_limit_bytes=4 << 20),
        name="blank",
    )(counts, after)


def surplus(counts, worker, owner, base, half, k):
    core = lax.rem(owner, 2)
    even = owner - core
    item = jnp.where(core == 1, (k + half) % (2 * half), k)
    first = jnp.maximum(counts[even, worker] - base, 0)
    second = jnp.maximum(counts[even + 1, worker] - base, 0)
    slot = base + jnp.where(item < first, item, item - first)
    return jnp.where(item < first, even, even + 1), slot, item < first + second


def pack_kernel(base, counts, own, twin, out):
    worker, me = lax.axis_index("dp"), lax.axis_index("mp")
    for k in range(out.shape[0]):
        owner, slot, _ = surplus(counts, worker, me, base, out.shape[0] // 2, k)
        at = jnp.clip(slot - base, 0, own.shape[0] - 1)

        @pl.when(owner == me)
        def _():
            out[k] = own[at]

        @pl.when(owner != me)
        def _():
            out[k] = twin[at]


def pack_call(counts, own, twin, base, room):
    return pl.pallas_call(
        functools.partial(pack_kernel, base),
        out_shape=jax.ShapeDtypeStruct((room,) + own.shape[1:], BF16),
        in_specs=[pl.BlockSpec(memory_space=SMEM)] + [pl.BlockSpec(memory_space=VMEM)] * 2,
        out_specs=pl.BlockSpec(memory_space=VMEM),
        cost_estimate=pl.CostEstimate(
            flops=0, bytes_accessed=2 * room * own.shape[1] * own.shape[2] * 2, transcendentals=0
        ),
        compiler_params=pltpu.CompilerParams(vmem_limit_bytes=8 << 20),
        name="pack",
    )(counts, own, twin)


def apply_kernel(spec, stream, counts, grads, *refs):
    count = len(spec)
    blocks = refs[:count]
    out, obuf, osem = refs[count : count + 3]
    me = lax.axis_index("mp")
    worker = lax.axis_index("dp")
    owners, slots = grads.shape[0], grads.shape[1]
    core = lax.rem(me, 2)
    flat = []
    for ref, (hops, flip, swap, first, half) in zip(blocks, spec):
        side = 1 - core if flip else core
        owner = me - core + side + lax.rem(2 * owners + hops * 2 * (2 * side - 1), owners)
        owner = jnp.where(owner >= owners, owner - owners, owner)
        if swap:
            owner = owner + 1 - 2 * lax.rem(owner, 2)
        for k in range(ref.shape[0]):
            if half:
                source, slot, live = surplus(counts, worker, owner, first, half, k)
                slot = jnp.minimum(slot, slots - 1)
            else:
                source, slot = owner, first + k
                live = slot < counts[owner, worker]
            flat.append((ref, k, source, slot, live, len(flat)))

    def store(owner, slot, i):
        return pltpu.make_async_copy(obuf.at[i], out.at[owner, slot], osem.at[i])

    if stream:
        gbuf, gsem = refs[count + 3 :]

        def load(owner, slot, i):
            return pltpu.make_async_copy(grads.at[owner, slot], gbuf.at[i], gsem.at[i])

        for _, _, owner, slot, live, i in flat:
            pl.when(live)(load(owner, slot, i).start)

    for g in range(0, len(flat), 4):
        group = flat[g : g + 4]
        if stream:
            for _, _, owner, slot, live, i in group:
                pl.when(live)(load(owner, slot, i).wait)
        values = [
            dot(ref[k], gbuf[i] if stream else grads[owner, slot]).astype(BF16)
            for ref, k, owner, slot, _, i in group
        ]
        for (_, _, _, _, _, i), value in zip(group, values):
            obuf[i] = value
        for _, _, owner, slot, live, i in group:
            pl.when(live)(store(owner, slot, i).start)

    for _, _, owner, slot, live, i in flat:
        pl.when(live)(store(owner, slot, i).wait)


def apply_call(counts, grads, pieces, result, stream=False):
    spec = [piece[1:] for piece in pieces]
    blocks = [piece[0] for piece in pieces]
    total = sum(block.shape[0] for block in blocks)
    order = grads.shape[-1]
    anyspec = pl.BlockSpec(memory_space=pltpu.HBM)
    buffers = [pltpu.VMEM((total, order, order), BF16), pltpu.SemaphoreType.DMA((total,))]

    def body(counts, grads, *refs):
        refs = refs[: len(blocks)] + refs[len(blocks) + 1 :]
        apply_kernel(spec, stream, counts, grads, *refs)

    return pl.pallas_call(
        body,
        out_shape=jax.ShapeDtypeStruct(grads.shape, BF16),
        in_specs=[pl.BlockSpec(memory_space=SMEM), anyspec if stream else pl.BlockSpec(memory_space=VMEM)]
        + [pl.BlockSpec(memory_space=VMEM)] * len(blocks)
        + [anyspec],
        out_specs=anyspec,
        scratch_shapes=buffers * (2 if stream else 1),
        input_output_aliases={2 + len(blocks): 0},
        cost_estimate=pl.CostEstimate(
            flops=total * 2 * order**3, bytes_accessed=total * order * order * 4, transcendentals=0
        ),
        compiler_params=pltpu.CompilerParams(vmem_limit_bytes=16 << 20),
        name="apply",
    )(counts, grads, *blocks, result)


def spread(size, half, own_a, stats, roots, counts, grads):
    ring = [(i, (i + 2 - 4 * (i % 2)) % size) for i in range(size)]
    pair = [(i, i ^ 1) for i in range(size)]

    def move(block, pairs, name):
        with jax.named_scope("s_" + name):
            return lax.ppermute(block, "mp", pairs)

    base = own_a.shape[0]
    join = jnp.concatenate
    tie = lambda *values: lax.optimization_barrier(values)
    near_a = move(own_a, ring, "near_a")
    twin_a = move(own_a, pair, "twin_a")
    near_b = move(twin_a, ring, "near_b")
    own_b, = newton_call(stats, roots, base, stats.shape[1] - base)
    twin_b = move(own_b, pair, "twin_b")
    near_a, own_b, twin_b = tie(near_a, own_b, twin_b)
    extra = pack_call(counts, own_b, twin_b, base, 2 * half)
    near_c = move(extra, ring, "near_c")
    result = blank_call(counts, grads, extra)
    near_b, own_b, far_in = tie(near_b, own_b, near_a)
    far_a = move(far_in, ring, "far_a")
    twin_near = move(far_in, pair, "twin_near")
    result = apply_call(
        counts,
        grads,
        [
            (own_a, 0, 0, 0, 0, 0),
            (own_b, 0, 0, 0, base, 0),
            (twin_a, 0, 1, 0, 0, 0),
            (twin_b, 0, 1, 0, base, 0),
        ],
        result,
        True,
    )
    near_c, far_a, twin_near, result = tie(near_c, far_a, twin_near, result)
    far_c = move(near_c[:half], ring, "far_c")
    twin_c = move(join([near_b, near_c, far_a]), pair, "twin_c")
    result = apply_call(
        counts,
        grads,
        [
            (near_a, 1, 0, 0, 0, 0),
            (near_b, 1, 0, 1, 0, 0),
            (near_c, 1, 0, 0, base, half),
            (far_a, 2, 0, 0, 0, 0),
            (twin_near, 1, 1, 0, 0, 0),
        ],
        result,
    )
    twin_c, result = tie(twin_c, result)
    result = apply_call(
        counts,
        grads,
        [
            (twin_c[:base], 1, 1, 1, 0, 0),
            (twin_c[base : base + 2 * half], 1, 1, 0, base, half),
            (twin_c[base + 2 * half :], 2, 1, 0, 0, 0),
        ],
        result,
    )
    far_c, result = tie(far_c, result)
    twin_far = move(far_c, pair, "twin_far")
    return apply_call(
        counts, grads, [(far_c, 2, 0, 0, base, half), (twin_far, 2, 1, 0, base, half)], result
    )


def local(size, stats, roots, counts, grads):
    hbm = lambda value: pltpu.with_memory_space_constraint(value, pltpu.HBM)
    stats, roots = hbm(stats), hbm(roots)
    base = stats.shape[1] // 2
    own_a, busiest = newton_call(stats, roots, 0, base, counts)
    halves = (2, 3, 4)
    branches = [functools.partial(spread, size, half) for half in halves]
    index = sum((busiest[0] > 2 * half).astype(jnp.int32) for half in halves[:-1])
    return lax.switch(index, branches, own_a, stats, roots, counts, grads)


def solution(mesh):
    return jax.shard_map(
        functools.partial(local, mesh.shape["mp"]),
        mesh=mesh,
        in_specs=(
            P("mp", "dp", None, None),
            P("mp", "dp", None, None),
            P(),
            P(None, "dp", None, "mp"),
        ),
        out_specs=P(None, "dp", None, "mp"),
        check_vma=False,
    )
```
